32 devices in a mesh: tm: 16 (over z, y, x), feat: 2 (over core).
Axes of the slice: x: 2, y: 2, z: 4, core: 2. Of those that a mesh axis runs over, the one named last changes fastest.
Arguments:
- margins: float32 [32, 24576], P('feat', 'tm'), may hold values from -6 to 256
- events: int32 [32, 24576], P('feat', 'tm'), may hold values 0 or 1
- tie_group: int32 [24576], P('tm'), may hold values from 0 to 24575, as said below
- in_node: int32 [24576], P('tm'), may hold values 0 or 1
- bins: int32 [512, 24576], P('feat', 'tm'), may hold values from 0 to 255
Outputs:
- grad: bfloat16 [32, 24576], P('feat', 'tm')
- hess: bfloat16 [32, 24576], P('feat', 'tm')
- gain: float32 [2, 256, 256], P('feat', 'tm')
The draws below stay inside these ranges and needn't reach their ends.
Inputs may be any that keep to these rules, and one draw needn't show every extreme that they name: `tie_group`: group ids never fall; a group's id is the position of its first row; a new group begins at the first row of each block of 1536 rows and at the last row, so no group holds rows of two devices.
All inputs are finite; a program needn't handle non-finite values. No bound on the sum of `events` or of `in_node` on one device may be relied on, other than what follows from the above.
Results may differ from the reference program's by a relative error of at most 0.0034.
Values may be sent and summed in bfloat16 or wider, within the bound.
No kernel may reach another device: no remote copies, remote signals or barrier semaphores. Data moves between devices by JAX's collectives and lax.ppermute only.
A program may use at most 128 MiB of HBM per device.

```python
import jax
import jax.numpy as jnp
from jax import lax

FEATURES = 512
BINS = 256
ENDP = 32
ROWS_DEV = 1536
ROWS = 24576
GROUPS = 2
GROUP_WIDTH = 256


def draw_margins(key, part):
    base_key = jax.random.fold_in(key, 0)
    return jnp.clip(jax.random.normal(base_key, (ENDP, ROWS), jnp.float32), -6.0, 6.0)


def draw_tie_group(key, part):
    start_draw = jax.random.randint(key, (ROWS,), 0, 8)
    position = jnp.arange(ROWS, dtype=jnp.int32)
    opens = jnp.logical_or(start_draw == 0, position % ROWS_DEV == 0)
    opens = jnp.logical_or(opens, position == ROWS - 1)
    return lax.cummax(jnp.where(opens, position, 0).astype(jnp.int32), axis=0)


def plant(result, stream_key, smallest, largest):
    place = [jax.random.randint(jax.random.fold_in(stream_key, axis), (), 0, length) for axis, length in enumerate(result.shape)]
    widest = result.shape.index(max(result.shape))
    next_to = place[:widest] + [(place[widest] + 1) % result.shape[widest]] + place[widest + 1:]
    return result.at[tuple(place)].set(smallest).at[tuple(next_to)].set(largest)


def setup_inputs(seed: int = 0) -> dict:
    splits = jax.random.split(jax.random.key(seed), 6)
    margins = draw_margins(jax.random.fold_in(splits[5], 71), 0)
    events = plant((jax.random.randint(splits[1], (ENDP, ROWS), 0, 3) < 1).astype(jnp.int32), jax.random.fold_in(splits[1], 1), 0, 1)
    tie_group = draw_tie_group(jax.random.fold_in(splits[5], 71), 0)
    in_node = plant((jax.random.randint(splits[3], (ROWS,), 0, 2) < 1).astype(jnp.int32), jax.random.fold_in(splits[3], 1), 0, 1)
    bins = plant(jax.random.randint(splits[4], (FEATURES, ROWS), 0, BINS), jax.random.fold_in(splits[4], 1), 0, BINS - 1).astype(jnp.int32)
    return dict(margins=margins, events=events, tie_group=tie_group, in_node=in_node, bins=bins)


log_floor = -1.0e30


def log_add(earlier, later):
    peak = jnp.maximum(earlier[0], later[0])
    return (peak, earlier[1] * jnp.exp(earlier[0] - peak) + later[1] * jnp.exp(later[0] - peak))


def log_add_pair(earlier, later):
    peak = jnp.maximum(earlier[0], later[0])
    early_scale = jnp.exp(earlier[0] - peak)
    late_scale = jnp.exp(later[0] - peak)
    return (peak, earlier[1] * early_scale + later[1] * late_scale,
            earlier[2] * early_scale * early_scale + later[2] * late_scale * late_scale)


def group_bounds(tie_group):
    length = tie_group.shape[0]
    position = jnp.arange(length, dtype=jnp.int32)
    change = tie_group[1:] != tie_group[:-1]
    group_open = jnp.concatenate([jnp.ones((1,), jnp.bool_), change])
    group_close = jnp.concatenate([change, jnp.ones((1,), jnp.bool_)])
    start_pos = lax.cummax(jnp.where(group_open, position, 0).astype(jnp.int32), axis=0)
    end_pos = lax.cummin(jnp.where(group_close, position, length - 1).astype(jnp.int32), axis=0, reverse=True)
    return start_pos, end_pos


def split_gain(histogram):
    left = jnp.cumsum(histogram, axis=3)
    whole = left[:, :, :, -1:]
    right = whole - left

    def ratio_term(portion):
        return portion[:, 0] * portion[:, 0] / (portion[:, 1] + 1.0)

    return jnp.mean(ratio_term(left) + ratio_term(right) - ratio_term(whole), axis=1)


def reference(margins, events, tie_group, in_node, bins):
    start_pos, end_pos = group_bounds(tie_group)
    unit_mass = jnp.ones_like(margins)
    risk_max, risk_sum = lax.associative_scan(log_add, (margins, unit_mass), reverse=True, axis=1)
    risk_log = jnp.take(risk_max + jnp.log(risk_sum), start_pos, axis=1)
    happened = events == 1
    event_mass = happened.astype(jnp.float32)
    event_log = jnp.where(happened, -risk_log, log_floor)
    event_max, first_sum, second_sum = lax.associative_scan(log_add_pair, (event_log, event_mass, event_mass), axis=1)
    event_max = jnp.take(event_max, end_pos, axis=1)
    first_sum = jnp.take(first_sum, end_pos, axis=1)
    second_sum = jnp.take(second_sum, end_pos, axis=1)
    scaled = jnp.exp(margins + event_max)
    grad = (scaled * first_sum - event_mass).astype(jnp.bfloat16)
    hess = (scaled * first_sum - scaled * scaled * second_sum).astype(jnp.bfloat16)
    chosen = (in_node == 1)[None, :]
    zero = jnp.zeros_like(grad)
    pairs = jnp.stack([jnp.where(chosen, grad, zero), jnp.where(chosen, hess, zero)]).astype(jnp.float32)
    pairs = pairs.reshape(2 * ENDP, ROWS).T

    def one_feature(code_row):
        return jax.ops.segment_sum(pairs, code_row, num_segments=BINS)

    histogram = lax.map(one_feature, bins)
    histogram = histogram.reshape(FEATURES, BINS, 2, ENDP).transpose(0, 2, 3, 1)
    gain = split_gain(histogram)
    return grad, hess, gain.reshape(GROUPS, GROUP_WIDTH, BINS)
```

```python
import functools

import jax
import jax.numpy as jnp
from jax import lax
from jax.experimental import pallas as pl
from jax.experimental.pallas import tpu as pltpu
from jax.sharding import PartitionSpec as P

BINS = 256
HALF = BINS // 2
LANES = 128
log_floor = -1e30
NT = (((1,), (1,)), ((), ()))
f32 = jnp.float32
bf16 = jnp.bfloat16


def ahead(x, step, fill):
    length = x.shape[1]
    pad = jnp.full((x.shape[0], step), fill, x.dtype)
    if step % LANES == 0:
        return jnp.concatenate([x[:, step:], pad], axis=1)
    lane = lax.broadcasted_iota(jnp.int32, x.shape, 1)
    return jnp.where(lane < length - step, pltpu.roll(x, length - step, 1), fill)


def behind(x, step, fill):
    length = x.shape[1]
    pad = jnp.full((x.shape[0], step), fill, x.dtype)
    if step % LANES == 0:
        return jnp.concatenate([pad, x[:, : length - step]], axis=1)
    lane = lax.broadcasted_iota(jnp.int32, x.shape, 1)
    return jnp.where(lane >= step, pltpu.roll(x, step, 1), fill)


def steps(length):
    step = 1
    while step < length:
        yield step
        step *= 2


def log_sum(a, b):
    peak = jnp.maximum(a, b)
    return peak + jnp.log(1.0 + jnp.exp(-jnp.abs(a - b)))


def risk_kernel(margins_ref, tie_ref, local_ref, total_ref):
    peak = margins_ref[...]
    length = peak.shape[1]
    mass = jnp.ones_like(peak)
    for step in steps(length):
        far_peak = ahead(peak, step, log_floor)
        far_mass = ahead(mass, step, 0.0)
        gap = peak - far_peak
        shrink = jnp.exp(-jnp.abs(gap))
        mass = jnp.where(gap >= 0, mass + far_mass * shrink, mass * shrink + far_mass)
        peak = jnp.maximum(peak, far_peak)
    risk = peak + jnp.log(mass)
    total_ref[...] = jnp.broadcast_to(risk[:, 0:1], (risk.shape[0], LANES))
    tie = jnp.broadcast_to(tie_ref[...], risk.shape)
    lane = lax.broadcasted_iota(jnp.int32, risk.shape, 1)
    opens = (lane == 0) | (tie != pltpu.roll(tie, 1, 1))
    filled = jnp.where(opens, risk, -log_floor)
    for step in steps(length):
        filled = jnp.minimum(filled, behind(filled, step, -log_floor))
    local_ref[...] = filled


def carried(place, parts, later, endpoints):
    count = parts.shape[0] // endpoints
    held = [parts[k * endpoints : (k + 1) * endpoints] for k in range(count)]
    held = [jnp.where((place < k) if later else (place > k), h, log_floor) for k, h in enumerate(held)]
    peak = functools.reduce(jnp.maximum, held)
    mass = functools.reduce(jnp.add, [jnp.exp(h - peak) for h in held])
    return jnp.where(peak > 0.5 * log_floor, peak + jnp.log(mass), log_floor)


def event_kernel(place_ref, local_ref, parts_ref, events_ref, tie_ref, first_ref, second_ref, total_ref):
    local = local_ref[...]
    endpoints, length = local.shape
    carry = carried(place_ref[0], parts_ref[...], True, endpoints)
    risk = log_sum(local, carry[:, 0:1])
    happened = events_ref[...] == 1
    peak = jnp.where(happened, -risk, log_floor)
    first = happened.astype(f32)
    second = first
    for step in steps(length):
        far_peak = behind(peak, step, log_floor)
        far_first = behind(first, step, 0.0)
        far_second = behind(second, step, 0.0)
        gap = peak - far_peak
        shrink = jnp.exp(-jnp.abs(gap))
        near = gap >= 0
        square = shrink * shrink
        first = jnp.where(near, first + far_first * shrink, first * shrink + far_first)
        second = jnp.where(near, second + far_second * square, second * square + far_second)
        peak = jnp.maximum(peak, far_peak)
    some = first > 0
    first_log = jnp.where(some, peak + jnp.log(first), log_floor)
    second_log = jnp.where(some, 2.0 * peak + jnp.log(second), log_floor)
    end = length - 1
    total_ref[0:endpoints] = jnp.broadcast_to(first_log[:, end:], (endpoints, LANES))
    total_ref[endpoints:] = jnp.broadcast_to(second_log[:, end:], (endpoints, LANES))
    tie = jnp.broadcast_to(tie_ref[...], local.shape)
    lane = lax.broadcasted_iota(jnp.int32, local.shape, 1)
    closes = (lane == end) | (tie != pltpu.roll(tie, length - 1, 1))
    first_fill = jnp.where(closes, first_log, -log_floor)
    second_fill = jnp.where(closes, second_log, -log_floor)
    for step in steps(length):
        first_fill = jnp.minimum(first_fill, ahead(first_fill, step, -log_floor))
        second_fill = jnp.minimum(second_fill, ahead(second_fill, step, -log_floor))
    first_ref[...] = first_fill
    second_ref[...] = second_fill


def grad_kernel(place_ref, margins_ref, events_ref, node_ref, first_ref, second_ref, parts_ref, grad_ref, hess_ref, pair_ref):
    margins = margins_ref[...]
    endpoints = margins.shape[0]
    carry = carried(place_ref[0], parts_ref[...], False, 2 * endpoints)
    first_log = log_sum(first_ref[...], carry[0:endpoints, 0:1])
    second_log = log_sum(second_ref[...], carry[endpoints:, 0:1])
    first = jnp.exp(margins + first_log)
    second = jnp.exp(2.0 * margins + second_log)
    grad = first - (events_ref[...] == 1).astype(f32)
    hess = first - second
    grad_ref[...] = grad.astype(bf16)
    hess_ref[...] = hess.astype(bf16)
    chosen = jnp.broadcast_to(node_ref[...], margins.shape) == 1
    pair_ref[0:endpoints] = jnp.where(chosen, grad, 0.0).astype(bf16)
    pair_ref[endpoints:] = jnp.where(chosen, hess, 0.0).astype(bf16)


def hist_kernel(blocks, feature_count, order_ref, bins_ref, pairs_ref, gain_ref, sums_ref):
    block = pl.program_id(0)
    channels = pairs_ref.shape[1]
    length = pairs_ref.shape[2]

    @pl.when(block == 0)
    def _():
        sums_ref[...] = jnp.zeros_like(sums_ref)

    level = lax.broadcasted_iota(jnp.int32, (HALF, length), 0).astype(bf16)
    pairs = pairs_ref[0]
    nothing = jnp.zeros_like(pairs)
    codes = bins_ref[0]
    upper = codes >= bf16(HALF)
    low = jnp.where(upper, codes - bf16(HALF), codes)
    high = jnp.where(upper, bf16(1), bf16(0))
    for f in range(feature_count):
        up = jnp.broadcast_to(high[f : f + 1], pairs.shape) == bf16(1)
        left = jnp.concatenate([jnp.where(up, nothing, pairs), jnp.where(up, pairs, nothing)], axis=0)
        reach = jnp.where(level >= low[f : f + 1], bf16(1), bf16(0))
        sums_ref[f] += lax.dot_general(left, reach, NT, preferred_element_type=f32)

    @pl.when(block == blocks - 1)
    def _():
        quarter = channels // 4

        def split(x):
            grad = jnp.concatenate([x[0:quarter], x[2 * quarter : 3 * quarter]], axis=0)
            hess = jnp.concatenate([x[quarter : 2 * quarter], x[3 * quarter :]], axis=0)
            return grad, hess

        def part(x):
            grad, hess = split(x)
            return grad * grad / (hess + 1.0)

        for f in range(feature_count):
            lower = sums_ref[f, 0:channels]
            under = lower[:, HALF - 1 :]
            uppers = sums_ref[f, channels:] + under
            whole = uppers[:, HALF - 1 :]
            whole_part = part(whole)
            for side, left in enumerate((lower, uppers)):
                value = part(left) + part(whole - left) - whole_part
                gain_ref[f : f + 1, side * HALF : (side + 1) * HALF] = jnp.mean(value, axis=0, keepdims=True)


def call(kernel, out_shape, name, **kw):
    return pl.pallas_call(kernel, out_shape=out_shape, name=name, **kw)


def shape(*dims, dtype=f32):
    return jax.ShapeDtypeStruct(dims, dtype)


VMEM = pl.BlockSpec(memory_space=pltpu.VMEM)
SMEM = pl.BlockSpec(memory_space=pltpu.SMEM)


def gather_rows(mine, devices):
    place = lax.axis_index("tm")
    if devices % 4 or devices > 16:
        return lax.all_gather(mine, "tm"), jnp.arange(devices, dtype=jnp.int32)
    planes = devices // 4
    column = [mine]
    origin = [place]
    for d in range(1, planes):
        ring = [(i, (i + 4 * d) % devices) for i in range(devices)]
        column.append(lax.ppermute(mine, "tm", ring))
        origin.append((place + devices - 4 * d) % devices)
    column = jnp.stack(column)
    origin = jnp.stack(origin)
    every = [column]
    order = [origin]
    for d in range(1, 4):
        every.append(lax.ppermute(column, "tm", [(i, i ^ d) for i in range(devices)]))
        order.append(origin ^ d)
    return jnp.concatenate(every, axis=0), jnp.concatenate(order)


def on_device(devices, margins, events, tie_group, in_node, bins):
    endpoints, length = margins.shape
    place = lax.axis_index("tm")
    here = place[None].astype(jnp.int32)
    tie = tie_group[None]
    mine = bins.shape[0] // devices
    codes = lax.all_to_all(bins.astype(bf16).reshape(devices, mine, length), "tm", 0, 0)

    def exchange(total):
        rows = total.shape[0]
        sent = lax.all_to_all(jnp.broadcast_to(total[None], (devices, rows, LANES)), "tm", 0, 0)
        return sent.reshape(devices * rows, LANES)

    local, total = call(
        risk_kernel, (shape(endpoints, length), shape(endpoints, LANES)), "risk",
        in_specs=[VMEM] * 2, out_specs=(VMEM,) * 2,
    )(margins, tie)
    first, second, total = call(
        event_kernel,
        (shape(endpoints, length), shape(endpoints, length), shape(2 * endpoints, LANES)), "events",
        in_specs=[SMEM] + [VMEM] * 4, out_specs=(VMEM,) * 3,
    )(here, local, exchange(total), events, tie)
    grad, hess, pairs = call(
        grad_kernel,
        (
            shape(endpoints, length, dtype=bf16),
            shape(endpoints, length, dtype=bf16),
            shape(2 * endpoints, length, dtype=bf16),
        ), "grads",
        in_specs=[SMEM] + [VMEM] * 6, out_specs=(VMEM,) * 3,
    )(here, margins, events, in_node[None], first, second, exchange(total))

    rows, order = gather_rows(pairs, devices)
    other = lax.ppermute(rows, "feat", [(0, 1), (1, 0)])
    rows = jnp.concatenate([rows, other], axis=1)

    gain = call(
        functools.partial(hist_kernel, devices, mine),
        shape(mine, BINS), "hist",
        grid_spec=pltpu.PrefetchScalarGridSpec(
            num_scalar_prefetch=1,
            grid=(devices,),
            in_specs=[
                pl.BlockSpec((1, mine, length), lambda i, order: (order[i], 0, 0)),
                pl.BlockSpec((1, 4 * endpoints, length), lambda i, order: (i, 0, 0)),
            ],
            out_specs=pl.BlockSpec((mine, BINS), lambda i, order: (0, 0)),
            scratch_shapes=[pltpu.VMEM((mine, 8 * endpoints, HALF), f32)],
        ),
        compiler_params=pltpu.CompilerParams(dimension_semantics=("arbitrary",), vmem_limit_bytes=48 << 20),
    )(order, codes, rows)
    return (grad, hess, gain[None])


def solution(mesh):
    in_specs = (P("feat", "tm"), P("feat", "tm"), P("tm"), P("tm"), P("feat", "tm"))
    out_specs = (P("feat", "tm"), P("feat", "tm"), P("feat", "tm", None))
    return jax.shard_map(
        functools.partial(on_device, mesh.shape["tm"]),
        mesh=mesh, in_specs=in_specs, out_specs=out_specs, check_vma=False,
    )
```

```python
import functools

import jax
import jax.numpy as jnp
from jax import lax
from jax.experimental import pallas as pl
from jax.experimental.pallas import tpu as pltpu
from jax.sharding import PartitionSpec as P

BINS = 256
HALF = BINS // 2
LANES = 128
log_floor = -1e30
NT = (((1,), (1,)), ((), ()))
f32 = jnp.float32
bf16 = jnp.bfloat16


def ahead(x, step, fill):
    length = x.shape[1]
    pad = jnp.full((x.shape[0], step), fill, x.dtype)
    if step % LANES == 0:
        return jnp.concatenate([x[:, step:], pad], axis=1)
    lane = lax.broadcasted_iota(jnp.int32, x.shape, 1)
    return jnp.where(lane < length - step, pltpu.roll(x, length - step, 1), fill)


def behind(x, step, fill):
    length = x.shape[1]
    pad = jnp.full((x.shape[0], step), fill, x.dtype)
    if step % LANES == 0:
        return jnp.concatenate([pad, x[:, : length - step]], axis=1)
    lane = lax.broadcasted_iota(jnp.int32, x.shape, 1)
    return jnp.where(lane >= step, pltpu.roll(x, step, 1), fill)


def steps(length):
    step = 1
    while step < length:
        yield step
        step *= 2


def log_sum(a, b):
    peak = jnp.maximum(a, b)
    return peak + jnp.log(1.0 + jnp.exp(-jnp.abs(a - b)))


def risk_kernel(margins_ref, tie_ref, local_ref, total_ref):
    peak = margins_ref[...]
    length = peak.shape[1]
    mass = jnp.ones_like(peak)
    for step in steps(length):
        far_peak = ahead(peak, step, log_floor)
        far_mass = ahead(mass, step, 0.0)
        gap = peak - far_peak
        shrink = jnp.exp(-jnp.abs(gap))
        mass = jnp.where(gap >= 0, mass + far_mass * shrink, mass * shrink + far_mass)
        peak = jnp.maximum(peak, far_peak)
    risk = peak + jnp.log(mass)
    total_ref[...] = jnp.broadcast_to(risk[:, 0:1], (risk.shape[0], LANES))
    tie = jnp.broadcast_to(tie_ref[...], risk.shape)
    lane = lax.broadcasted_iota(jnp.int32, risk.shape, 1)
    opens = (lane == 0) | (tie != pltpu.roll(tie, 1, 1))
    filled = jnp.where(opens, risk, -log_floor)
    for step in steps(length):
        filled = jnp.minimum(filled, behind(filled, step, -log_floor))
    local_ref[...] = filled


def carried(place, parts, later, endpoints):
    count = parts.shape[0] // endpoints
    held = [parts[k * endpoints : (k + 1) * endpoints] for k in range(count)]
    held = [jnp.where((place < k) if later else (place > k), h, log_floor) for k, h in enumerate(held)]
    peak = functools.reduce(jnp.maximum, held)
    mass = functools.reduce(jnp.add, [jnp.exp(h - peak) for h in held])
    return jnp.where(peak > 0.5 * log_floor, peak + jnp.log(mass), log_floor)


def event_kernel(place_ref, local_ref, parts_ref, events_ref, tie_ref, first_ref, second_ref, total_ref):
    local = local_ref[...]
    endpoints, length = local.shape
    carry = carried(place_ref[0], parts_ref[...], True, endpoints)
    risk = log_sum(local, carry[:, 0:1])
    happened = events_ref[...] == 1
    peak = jnp.where(happened, -risk, log_floor)
    first = happened.astype(f32)
    second = first
    for step in steps(length):
        far_peak = behind(peak, step, log_floor)
        far_first = behind(first, step, 0.0)
        far_second = behind(second, step, 0.0)
        gap = peak - far_peak
        shrink = jnp.exp(-jnp.abs(gap))
        near = gap >= 0
        square = shrink * shrink
        first = jnp.where(near, first + far_first * shrink, first * shrink + far_first)
        second = jnp.where(near, second + far_second * square, second * square + far_second)
        peak = jnp.maximum(peak, far_peak)
    some = first > 0
    first_log = jnp.where(some, peak + jnp.log(first), log_floor)
    second_log = jnp.where(some, 2.0 * peak + jnp.log(second), log_floor)
    end = length - 1
    total_ref[0:endpoints] = jnp.broadcast_to(first_log[:, end:], (endpoints, LANES))
    total_ref[endpoints:] = jnp.broadcast_to(second_log[:, end:], (endpoints, LANES))
    tie = jnp.broadcast_to(tie_ref[...], local.shape)
    lane = lax.broadcasted_iota(jnp.int32, local.shape, 1)
    closes = (lane == end) | (tie != pltpu.roll(tie, length - 1, 1))
    first_fill = jnp.where(closes, first_log, -log_floor)
    second_fill = jnp.where(closes, second_log, -log_floor)
    for step in steps(length):
        first_fill = jnp.minimum(first_fill, ahead(first_fill, step, -log_floor))
        second_fill = jnp.minimum(second_fill, ahead(second_fill, step, -log_floor))
    first_ref[...] = first_fill
    second_ref[...] = second_fill


def grad_kernel(place_ref, margins_ref, events_ref, node_ref, first_ref, second_ref, parts_ref, grad_ref, hess_ref, pair_ref):
    margins = margins_ref[...]
    endpoints = margins.shape[0]
    carry = carried(place_ref[0], parts_ref[...], False, 2 * endpoints)
    first_log = log_sum(first_ref[...], carry[0:endpoints, 0:1])
    second_log = log_sum(second_ref[...], carry[endpoints:, 0:1])
    first = jnp.exp(margins + first_log)
    second = jnp.exp(2.0 * margins + second_log)
    grad = first - (events_ref[...] == 1).astype(f32)
    hess = first - second
    grad_ref[...] = grad.astype(bf16)
    hess_ref[...] = hess.astype(bf16)
    chosen = jnp.broadcast_to(node_ref[...], margins.shape) == 1
    pair_ref[0:endpoints] = jnp.where(chosen, grad, 0.0).astype(bf16)
    pair_ref[endpoints:] = jnp.where(chosen, hess, 0.0).astype(bf16)


def add_block(codes, pairs, sums_ref, feature_count):
    length = pairs.shape[1]
    level = lax.broadcasted_iota(jnp.int32, (HALF, length), 0).astype(bf16)
    nothing = jnp.zeros_like(pairs)
    upper = codes >= bf16(HALF)
    low = jnp.where(upper, codes - bf16(HALF), codes)
    high = jnp.where(upper, bf16(1), bf16(0))
    for f in range(feature_count):
        up = jnp.broadcast_to(high[f : f + 1], pairs.shape) == bf16(1)
        left = jnp.concatenate([jnp.where(up, nothing, pairs), jnp.where(up, pairs, nothing)], axis=0)
        reach = jnp.where(level >= low[f : f + 1], bf16(1), bf16(0))
        sums_ref[f] += lax.dot_general(left, reach, NT, preferred_element_type=f32)


def write_gain(sums_ref, gain_ref, feature_count, channels):
    quarter = channels // 4

    def part(x):
        grad = jnp.concatenate([x[0:quarter], x[2 * quarter : 3 * quarter]], axis=0)
        hess = jnp.concatenate([x[quarter : 2 * quarter], x[3 * quarter :]], axis=0)
        return grad * grad / (hess + 1.0)

    for f in range(feature_count):
        lower = sums_ref[f, 0:channels]
        under = lower[:, HALF - 1 :]
        uppers = sums_ref[f, channels:] + under
        whole = uppers[:, HALF - 1 :]
        whole_part = part(whole)
        for side, left in enumerate((lower, uppers)):
            value = part(left) + part(whole - left) - whole_part
            gain_ref[f : f + 1, side * HALF : (side + 1) * HALF] = jnp.mean(value, axis=0, keepdims=True)


def hist_kernel(blocks, feature_count, first, last, *refs):
    if first:
        codes_ref, mine_ref, other_ref, *outs = refs
    else:
        codes_ref, mine_ref, other_ref, before_ref, *outs = refs
    sums_ref = outs[-1]
    block = pl.program_id(0)

    @pl.when(block == 0)
    def _():
        sums_ref[...] = jnp.zeros_like(sums_ref) if first else before_ref[...]

    pairs = jnp.concatenate([mine_ref[0], other_ref[0]], axis=0)
    add_block(codes_ref[0], pairs, sums_ref, feature_count)
    if last:

        @pl.when(block == blocks - 1)
        def _():
            write_gain(sums_ref, outs[0], feature_count, pairs.shape[0])


def histogram(codes, mine, other, before, last):
    blocks, feature_count, length = codes.shape
    half = mine.shape[1]
    sums = (feature_count, 4 * half, HALF)
    operands = [codes, mine, other]
    in_specs = [
        pl.BlockSpec((1, feature_count, length), lambda i: (i, 0, 0)),
        pl.BlockSpec((1, half, length), lambda i: (i, 0, 0)),
        pl.BlockSpec((1, half, length), lambda i: (i, 0, 0)),
    ]
    whole = pl.BlockSpec(sums, lambda i: (0, 0, 0))
    if before is not None:
        operands.append(before)
        in_specs.append(whole)
    return pl.pallas_call(
        functools.partial(hist_kernel, blocks, feature_count, before is None, last),
        out_shape=shape(feature_count, BINS) if last else shape(*sums),
        grid=(blocks,),
        in_specs=in_specs,
        out_specs=pl.BlockSpec((feature_count, BINS), lambda i: (0, 0)) if last else whole,
        scratch_shapes=[pltpu.VMEM(sums, f32)] if last else [],
        input_output_aliases={3: 0} if before is not None and not last else {},
        name="hist",
        compiler_params=pltpu.CompilerParams(dimension_semantics=("arbitrary",), vmem_limit_bytes=32 << 20),
        cost_estimate=pl.CostEstimate(
            flops=blocks * feature_count * 2 * (4 * half) * HALF * length * 4,
            bytes_accessed=blocks * (feature_count + 2 * half) * length * 2,
            transcendentals=0,
        ),
    )(*operands)


def call(kernel, out_shape, name, **kw):
    return pl.pallas_call(kernel, out_shape=out_shape, name=name, **kw)


def shape(*dims, dtype=f32):
    return jax.ShapeDtypeStruct(dims, dtype)


VMEM = pl.BlockSpec(memory_space=pltpu.VMEM)
SMEM = pl.BlockSpec(memory_space=pltpu.SMEM)


def ring(devices, d):
    return [(i, (i + 4 * d) % devices) for i in range(devices)]


def flip(devices, d):
    return [(i, i ^ d) for i in range(devices)]


def swap(x):
    return lax.ppermute(x, "feat", [(0, 1), (1, 0)])


def pick(x, index, axis):
    return lax.dynamic_index_in_dim(x, index, axis, False)


def send_codes(codes, devices):
    planes = devices // 4
    place = lax.axis_index("tm")
    plane, column = place // 4, place % 4
    _, mine, length = codes.reshape(devices, -1, codes.shape[1]).shape
    codes = codes.reshape(planes, 4, mine, length)
    held = [pick(codes, plane, 0)]
    for d in range(1, planes):
        held.append(lax.ppermute(pick(codes, (plane + d) % planes, 0), "tm", ring(devices, d)))
    own = pick(held[0], column, 0)[None]
    near = jnp.stack([pick(h, column, 0) for h in held[1:]])
    far = [
        lax.ppermute(jnp.stack([pick(h, column ^ d, 0) for h in held]), "tm", flip(devices, d))
        for d in range(1, 4)
    ]
    return own, near, far


def spread(codes, pairs, devices):
    own, near, far = codes
    planes = devices // 4
    sums = histogram(own, pairs[None], swap(pairs)[None], None, False)
    column = [lax.ppermute(pairs, "tm", ring(devices, d)) for d in range(1, planes)]
    column = jnp.stack([pairs] + column)
    other = swap(column)
    sums = histogram(near, column[1:], other[1:], sums, False)
    for d in range(1, 4):
        there = lax.ppermute(column, "tm", flip(devices, d))
        sums = histogram(far[d - 1], there, swap(there), sums, d == 3)
    return sums


def spread_any(codes, pairs):
    rows = lax.all_gather(pairs, "tm")
    return histogram(codes, rows, swap(rows), None, True)


def on_device(devices, margins, events, tie_group, in_node, bins):
    endpoints, length = margins.shape
    place = lax.axis_index("tm")
    here = place[None].astype(jnp.int32)
    tie = tie_group[None]
    mine = bins.shape[0] // devices
    codes = bins.astype(bf16)
    if devices == 16:
        codes = send_codes(codes, devices)
    else:
        codes = lax.all_to_all(codes.reshape(devices, mine, length), "tm", 0, 0)

    def exchange(total):
        rows = total.shape[0]
        sent = lax.all_to_all(jnp.broadcast_to(total[None], (devices, rows, LANES)), "tm", 0, 0)
        return sent.reshape(devices * rows, LANES)

    local, total = call(
        risk_kernel, (shape(endpoints, length), shape(endpoints, LANES)), "risk",
        in_specs=[VMEM] * 2, out_specs=(VMEM,) * 2,
    )(margins, tie)
    first, second, total = call(
        event_kernel,
        (shape(endpoints, length), shape(endpoints, length), shape(2 * endpoints, LANES)), "events",
        in_specs=[SMEM] + [VMEM] * 4, out_specs=(VMEM,) * 3,
    )(here, local, exchange(total), events, tie)
    grad, hess, pairs = call(
        grad_kernel,
        (
            shape(endpoints, length, dtype=bf16),
            shape(endpoints, length, dtype=bf16),
            shape(2 * endpoints, length, dtype=bf16),
        ), "grads",
        in_specs=[SMEM] + [VMEM] * 6, out_specs=(VMEM,) * 3,
    )(here, margins, events, in_node[None], first, second, exchange(total))

    gain = spread(codes, pairs, devices) if devices == 16 else spread_any(codes, pairs)
    return (grad, hess, gain[None])


def solution(mesh):
    in_specs = (P("feat", "tm"), P("feat", "tm"), P("tm"), P("tm"), P("feat", "tm"))
    out_specs = (P("feat", "tm"), P("feat", "tm"), P("feat", "tm", None))
    return jax.shard_map(
        functools.partial(on_device, mesh.shape["tm"]),
        mesh=mesh, in_specs=in_specs, out_specs=out_specs, check_vma=False,
    )
```

```python
import functools

import jax
import jax.numpy as jnp
from jax import lax
from jax.experimental import pallas as pl
from jax.experimental.pallas import tpu as pltpu
from jax.sharding import PartitionSpec as P

BINS = 256
HALF = BINS // 2
LANES = 128
log_floor = -1e30
NT = (((1,), (1,)), ((), ()))
f32 = jnp.float32
bf16 = jnp.bfloat16


def ahead(x, step, fill):
    length = x.shape[1]
    pad = jnp.full((x.shape[0], step), fill, x.dtype)
    if step % LANES == 0:
        return jnp.concatenate([x[:, step:], pad], axis=1)
    lane = lax.broadcasted_iota(jnp.int32, x.shape, 1)
    return jnp.where(lane < length - step, pltpu.roll(x, length - step, 1), fill)


def behind(x, step, fill):
    length = x.shape[1]
    pad = jnp.full((x.shape[0], step), fill, x.dtype)
    if step % LANES == 0:
        return jnp.concatenate([pad, x[:, : length - step]], axis=1)
    lane = lax.broadcasted_iota(jnp.int32, x.shape, 1)
    return jnp.where(lane >= step, pltpu.roll(x, step, 1), fill)


def steps(length):
    step = 1
    while step < length:
        yield step
        step *= 2


def log_sum(a, b):
    peak = jnp.maximum(a, b)
    return peak + jnp.log(1.0 + jnp.exp(-jnp.abs(a - b)))


def share(total, total_ref):
    wide = jnp.broadcast_to(total, total_ref.shape[1:])
    for k in range(total_ref.shape[0]):
        total_ref[k] = wide


def share_row(total, total_ref):
    row = jnp.sum(jnp.where(diagonal((total.shape[0], LANES)), total, 0.0), axis=0, keepdims=True)
    for k in range(total_ref.shape[0]):
        total_ref[k] = row


def diagonal(like):
    return lax.broadcasted_iota(jnp.int32, like, 0) == lax.broadcasted_iota(jnp.int32, like, 1)


def risk_kernel(margins_ref, risk_ref, total_ref):
    peak = margins_ref[...]
    length = peak.shape[1]
    mass = jnp.ones_like(peak)
    for step in steps(length):
        far_peak = ahead(peak, step, log_floor)
        far_mass = ahead(mass, step, 0.0)
        gap = peak - far_peak
        shrink = jnp.exp(-jnp.abs(gap))
        mass = jnp.where(gap >= 0, mass + far_mass * shrink, mass * shrink + far_mass)
        peak = jnp.maximum(peak, far_peak)
    risk = peak + jnp.log(mass)
    share(risk[:, 0:1], total_ref)
    risk_ref[...] = risk


def tie_rows(tie_ref, like):
    return jnp.broadcast_to(tie_ref[...][None], like.shape)


def open_kernel(risk_ref, tie_ref, local_ref):
    risk = risk_ref[...]
    tie = tie_rows(tie_ref, risk)
    lane = lax.broadcasted_iota(jnp.int32, risk.shape, 1)
    opens = (lane == 0) | (tie != pltpu.roll(tie, 1, 1))
    filled = jnp.where(opens, risk, -log_floor)
    for step in steps(risk.shape[1]):
        filled = jnp.minimum(filled, behind(filled, step, -log_floor))
    local_ref[...] = filled


def carried_later(place, parts_ref):
    held = [jnp.where(place < k, parts_ref[k], log_floor) for k in range(parts_ref.shape[0])]
    peak = functools.reduce(jnp.maximum, held)
    mass = functools.reduce(jnp.add, [jnp.exp(h - peak) for h in held])
    return jnp.where(peak > 0.5 * log_floor, peak + jnp.log(mass), log_floor)[:, 0:1]


def carried_earlier(place, parts_ref, count):
    parts = jnp.concatenate([parts_ref[k] for k in range(parts_ref.shape[0])], axis=0)
    device = lax.broadcasted_iota(jnp.int32, parts.shape, 0)
    held = jnp.where(device < place, parts, log_floor)
    peak = jnp.max(held, axis=0, keepdims=True)
    mass = jnp.sum(jnp.exp(held - peak), axis=0, keepdims=True)
    row = jnp.where(peak > 0.5 * log_floor, peak + jnp.log(mass), log_floor)
    return jnp.sum(jnp.where(diagonal((count, LANES)), row, 0.0), axis=1, keepdims=True)


def event_kernel(place_ref, local_ref, parts_ref, events_ref, first_ref, second_ref, total_ref):
    local = local_ref[...]
    endpoints, length = local.shape
    risk = log_sum(local, carried_later(place_ref[0], parts_ref))
    happened = events_ref[...] == 1
    peak = jnp.where(happened, -risk, log_floor)
    first = happened.astype(f32)
    second = first
    for step in steps(length):
        far_peak = behind(peak, step, log_floor)
        far_first = behind(first, step, 0.0)
        far_second = behind(second, step, 0.0)
        gap = peak - far_peak
        shrink = jnp.exp(-jnp.abs(gap))
        near = gap >= 0
        square = shrink * shrink
        first = jnp.where(near, first + far_first * shrink, first * shrink + far_first)
        second = jnp.where(near, second + far_second * square, second * square + far_second)
        peak = jnp.maximum(peak, far_peak)
    some = first > 0
    first_log = jnp.where(some, peak + jnp.log(first), log_floor)
    second_log = jnp.where(some, 2.0 * peak + jnp.log(second), log_floor)
    end = length - 1
    share_row(jnp.concatenate([first_log[:, end:], second_log[:, end:]], axis=0), total_ref)
    first_ref[...] = first_log
    second_ref[...] = second_log


def close_kernel(first_ref, second_ref, tie_ref, first_out, second_out):
    first = first_ref[...]
    second = second_ref[...]
    tie = tie_rows(tie_ref, first)
    length = first.shape[1]
    lane = lax.broadcasted_iota(jnp.int32, first.shape, 1)
    closes = (lane == length - 1) | (tie != pltpu.roll(tie, length - 1, 1))
    first = jnp.where(closes, first, -log_floor)
    second = jnp.where(closes, second, -log_floor)
    for step in steps(length):
        first = jnp.minimum(first, ahead(first, step, -log_floor))
        second = jnp.minimum(second, ahead(second, step, -log_floor))
    first_out[...] = first
    second_out[...] = second


def grad_kernel(place_ref, margins_ref, events_ref, node_ref, first_ref, second_ref, parts_ref, grad_ref, hess_ref, pair_ref):
    margins = margins_ref[...]
    endpoints = margins.shape[0]
    carry = carried_earlier(place_ref[0], parts_ref, 2 * endpoints)
    first_log = log_sum(first_ref[...], carry[0:endpoints])
    second_log = log_sum(second_ref[...], carry[endpoints:])
    first = jnp.exp(margins + first_log)
    second = jnp.exp(2.0 * margins + second_log)
    grad = first - (events_ref[...] == 1).astype(f32)
    hess = first - second
    grad_ref[...] = grad.astype(bf16)
    hess_ref[...] = hess.astype(bf16)
    chosen = tie_rows(node_ref, margins) == 1
    pair_ref[0:endpoints] = jnp.where(chosen, grad, 0.0).astype(bf16)
    pair_ref[endpoints:] = jnp.where(chosen, hess, 0.0).astype(bf16)


def add_block(codes, pairs, sums_ref, feature_count):
    length = pairs.shape[1]
    level = lax.broadcasted_iota(jnp.int32, (HALF, length), 0).astype(bf16)
    nothing = jnp.zeros_like(pairs)
    upper = codes >= bf16(HALF)
    low = jnp.where(upper, codes - bf16(HALF), codes)
    high = jnp.where(upper, bf16(1), bf16(0))
    for f in range(feature_count):
        up = jnp.broadcast_to(high[f : f + 1], pairs.shape) == bf16(1)
        left = jnp.concatenate([jnp.where(up, nothing, pairs), jnp.where(up, pairs, nothing)], axis=0)
        reach = jnp.where(level >= low[f : f + 1], bf16(1), bf16(0))
        sums_ref[f] += lax.dot_general(left, reach, NT, preferred_element_type=f32)


def write_gain(sums_ref, gain_ref, feature_count, channels):
    quarter = channels // 4

    def part(x):
        grad = jnp.concatenate([x[0:quarter], x[2 * quarter : 3 * quarter]], axis=0)
        hess = jnp.concatenate([x[quarter : 2 * quarter], x[3 * quarter :]], axis=0)
        return grad * grad / (hess + 1.0)

    for f in range(feature_count):
        lower = sums_ref[f, 0:channels]
        under = lower[:, HALF - 1 :]
        uppers = sums_ref[f, channels:] + under
        whole = uppers[:, HALF - 1 :]
        whole_part = part(whole)
        for side, left in enumerate((lower, uppers)):
            value = part(left) + part(whole - left) - whole_part
            gain_ref[f : f + 1, side * HALF : (side + 1) * HALF] = jnp.mean(value, axis=0, keepdims=True)


def hist_kernel(blocks, feature_count, first, last, *refs):
    if first:
        codes_ref, mine_ref, other_ref, *outs = refs
    else:
        codes_ref, mine_ref, other_ref, before_ref, *outs = refs
    sums_ref = outs[-1]
    block = pl.program_id(0)

    @pl.when(block == 0)
    def _():
        sums_ref[...] = jnp.zeros_like(sums_ref) if first else before_ref[...]

    pairs = jnp.concatenate([mine_ref[0], other_ref[0]], axis=0)
    add_block(codes_ref[0], pairs, sums_ref, feature_count)
    if last:

        @pl.when(block == blocks - 1)
        def _():
            write_gain(sums_ref, outs[0], feature_count, pairs.shape[0])


def histogram(codes, mine, other, before, last):
    blocks, feature_count, length = codes.shape
    half = mine.shape[1]
    sums = (feature_count, 4 * half, HALF)
    operands = [codes, mine, other]
    in_specs = [
        pl.BlockSpec((1, feature_count, length), lambda i: (i, 0, 0)),
        pl.BlockSpec((1, half, length), lambda i: (i, 0, 0)),
        pl.BlockSpec((1, half, length), lambda i: (i, 0, 0)),
    ]
    whole = pl.BlockSpec(sums, lambda i: (0, 0, 0))
    if before is not None:
        operands.append(before)
        in_specs.append(whole)
    return pl.pallas_call(
        functools.partial(hist_kernel, blocks, feature_count, before is None, last),
        out_shape=shape(feature_count, BINS) if last else shape(*sums),
        grid=(blocks,),
        in_specs=in_specs,
        out_specs=pl.BlockSpec((feature_count, BINS), lambda i: (0, 0)) if last else whole,
        scratch_shapes=[pltpu.VMEM(sums, f32)] if last else [],
        input_output_aliases={3: 0} if before is not None and not last else {},
        name="hist",
        compiler_params=pltpu.CompilerParams(dimension_semantics=("arbitrary",), vmem_limit_bytes=20 << 20),
        cost_estimate=pl.CostEstimate(
            flops=blocks * feature_count * 2 * (4 * half) * HALF * length * 4,
            bytes_accessed=blocks * (feature_count + 2 * half) * length * 2,
            transcendentals=0,
        ),
    )(*operands)


def call(kernel, out_shape, name, *operands, place=False):
    single = isinstance(out_shape, jax.ShapeDtypeStruct)
    return pl.pallas_call(
        kernel,
        out_shape=out_shape,
        in_specs=([SMEM] if place else []) + [VMEM] * (len(operands) - place),
        out_specs=VMEM if single else (VMEM,) * len(out_shape),
        name=name,
        compiler_params=pltpu.CompilerParams(vmem_limit_bytes=12 << 20),
    )(*operands)


def shape(*dims, dtype=f32):
    return jax.ShapeDtypeStruct(dims, dtype)


VMEM = pl.BlockSpec(memory_space=pltpu.VMEM)
SMEM = pl.BlockSpec(memory_space=pltpu.SMEM)


def ring(devices, d):
    return [(i, (i + 4 * d) % devices) for i in range(devices)]


def flip(devices, d):
    return [(i, i ^ d) for i in range(devices)]


def swap(x):
    return lax.ppermute(x, "feat", [(0, 1), (1, 0)])


def pick(x, index, axis):
    return lax.dynamic_index_in_dim(x, index, axis, False)


def send_planes(codes, devices):
    planes = devices // 4
    plane = lax.axis_index("tm") // 4
    codes = codes.reshape(planes, 4, -1, codes.shape[1])
    held = [pick(codes, plane, 0)]
    for d in range(1, planes):
        held.append(lax.ppermute(pick(codes, (plane + d) % planes, 0), "tm", ring(devices, d)))
    return held


def spread(held, pairs, devices):
    planes = devices // 4
    here = lax.axis_index("tm") % 4
    column = [lax.ppermute(pairs, "tm", ring(devices, d)) for d in range(1, planes)]
    sums = histogram(pick(held[0], here, 0)[None], pairs[None], swap(pairs)[None], None, False)
    held, sums = lax.optimization_barrier((held, sums))
    near = jnp.stack([pick(h, here, 0) for h in held[1:]])
    far = [
        lax.ppermute(jnp.stack([pick(h, here ^ d, 0) for h in held]), "tm", flip(devices, d))
        for d in range(1, 4)
    ]
    far, *column, sums = lax.optimization_barrier((far, *column, sums))
    column = jnp.stack([pairs] + column)
    other = swap(column)
    there = [lax.ppermute(column, "tm", flip(devices, d)) for d in range(1, 4)]
    cut = planes - 2
    sums = histogram(near[:cut], column[1 : cut + 1], other[1 : cut + 1], sums, False)
    there[0], sums = lax.optimization_barrier((there[0], sums))
    back = swap(there[0])
    sums = histogram(near[cut:], column[cut + 1 :], other[cut + 1 :], sums, False)
    for d in range(1, 4):
        mine = there[d - 1]
        now = back
        if d < 3:
            there[d], sums = lax.optimization_barrier((there[d], sums))
            back = swap(there[d])
        sums = histogram(far[d - 1], mine, now, sums, d == 3)
    return sums


def spread_any(codes, pairs):
    rows = lax.all_gather(pairs, "tm")
    return histogram(codes, rows, swap(rows), None, True)


def on_device(devices, margins, events, tie_group, in_node, bins):
    endpoints, length = margins.shape
    here = lax.axis_index("tm")[None].astype(jnp.int32)
    mine = bins.shape[0] // devices
    rows = shape(endpoints, length)
    narrow = shape(endpoints, length, dtype=bf16)

    def exchange(total):
        return lax.all_to_all(total, "tm", 0, 0)

    risk, total = call(risk_kernel, (rows, shape(devices, endpoints, LANES)), "risk", margins)
    parts = exchange(total)
    local = call(open_kernel, rows, "opens", risk, tie_group)
    bins, local = lax.optimization_barrier((bins, local))
    codes = bins.astype(bf16)
    blocked = devices == 16
    if blocked:
        codes = send_planes(codes, devices)
    else:
        codes = lax.all_to_all(codes.reshape(devices, mine, length), "tm", 0, 0)
    first, second, total = call(
        event_kernel, (rows, rows, shape(devices, 1, LANES)), "events",
        here, local, parts, events, place=True,
    )
    parts = exchange(total)
    first, second = call(close_kernel, (rows, rows), "closes", first, second, tie_group)
    codes, parts = lax.optimization_barrier((codes, parts))
    grad, hess, pairs = call(
        grad_kernel, (narrow, narrow, shape(2 * endpoints, length, dtype=bf16)), "grads",
        here, margins, events, in_node, first, second, parts, place=True,
    )
    gain = spread(codes, pairs, devices) if blocked else spread_any(codes, pairs)
    return (grad, hess, gain[None])


def solution(mesh):
    in_specs = (P("feat", "tm"), P("feat", "tm"), P("tm"), P("tm"), P("feat", "tm"))
    out_specs = (P("feat", "tm"), P("feat", "tm"), P("feat", "tm", None))
    return jax.shard_map(
        functools.partial(on_device, mesh.shape["tm"]),
        mesh=mesh, in_specs=in_specs, out_specs=out_specs, check_vma=False,
    )
```

```python
import functools

import jax
import jax.numpy as jnp
from jax import lax
from jax.experimental import pallas as pl
from jax.experimental.pallas import tpu as pltpu
from jax.sharding import PartitionSpec as P

BINS = 256
HALF = BINS // 2
LANES = 128
log_floor = -1e30
NT = (((1,), (1,)), ((), ()))
f32 = jnp.float32
bf16 = jnp.bfloat16


def ahead(x, step, fill):
    length = x.shape[1]
    pad = jnp.full((x.shape[0], step), fill, x.dtype)
    if step % LANES == 0:
        return jnp.concatenate([x[:, step:], pad], axis=1)
    lane = lax.broadcasted_iota(jnp.int32, x.shape, 1)
    return jnp.where(lane < length - step, pltpu.roll(x, length - step, 1), fill)


def behind(x, step, fill):
    length = x.shape[1]
    pad = jnp.full((x.shape[0], step), fill, x.dtype)
    if step % LANES == 0:
        return jnp.concatenate([pad, x[:, : length - step]], axis=1)
    lane = lax.broadcasted_iota(jnp.int32, x.shape, 1)
    return jnp.where(lane >= step, pltpu.roll(x, step, 1), fill)


def steps(length):
    step = 1
    while step < length:
        yield step
        step *= 2


def log_sum(a, b):
    peak = jnp.maximum(a, b)
    return peak + jnp.log(1.0 + jnp.exp(-jnp.abs(a - b)))


def share(total, total_ref):
    wide = jnp.broadcast_to(total, total_ref.shape[1:])
    for k in range(total_ref.shape[0]):
        total_ref[k] = wide


def share_row(total, total_ref):
    row = jnp.sum(jnp.where(diagonal((total.shape[0], LANES)), total, 0.0), axis=0, keepdims=True)
    for k in range(total_ref.shape[0]):
        total_ref[k] = row


def diagonal(like):
    return lax.broadcasted_iota(jnp.int32, like, 0) == lax.broadcasted_iota(jnp.int32, like, 1)


def risk_kernel(margins_ref, risk_ref, total_ref):
    peak = margins_ref[...]
    length = peak.shape[1]
    mass = jnp.ones_like(peak)
    for step in steps(length):
        far_peak = ahead(peak, step, log_floor)
        far_mass = ahead(mass, step, 0.0)
        gap = peak - far_peak
        shrink = jnp.exp(-jnp.abs(gap))
        mass = jnp.where(gap >= 0, mass + far_mass * shrink, mass * shrink + far_mass)
        peak = jnp.maximum(peak, far_peak)
    risk = peak + jnp.log(mass)
    share(risk[:, 0:1], total_ref)
    risk_ref[...] = risk


def tie_rows(tie_ref, like):
    return jnp.broadcast_to(tie_ref[...][None], like.shape)


def open_kernel(risk_ref, tie_ref, local_ref):
    risk = risk_ref[...]
    tie = tie_rows(tie_ref, risk)
    lane = lax.broadcasted_iota(jnp.int32, risk.shape, 1)
    opens = (lane == 0) | (tie != pltpu.roll(tie, 1, 1))
    filled = jnp.where(opens, risk, -log_floor)
    for step in steps(risk.shape[1]):
        filled = jnp.minimum(filled, behind(filled, step, -log_floor))
    local_ref[...] = filled


def carried_later(place, parts_ref):
    held = [jnp.where(place < k, parts_ref[k], log_floor) for k in range(parts_ref.shape[0])]
    peak = functools.reduce(jnp.maximum, held)
    mass = functools.reduce(jnp.add, [jnp.exp(h - peak) for h in held])
    return jnp.where(peak > 0.5 * log_floor, peak + jnp.log(mass), log_floor)[:, 0:1]


def carried_earlier(place, parts_ref, count):
    parts = jnp.concatenate([parts_ref[k] for k in range(parts_ref.shape[0])], axis=0)
    device = lax.broadcasted_iota(jnp.int32, parts.shape, 0)
    held = jnp.where(device < place, parts, log_floor)
    peak = jnp.max(held, axis=0, keepdims=True)
    mass = jnp.sum(jnp.exp(held - peak), axis=0, keepdims=True)
    row = jnp.where(peak > 0.5 * log_floor, peak + jnp.log(mass), log_floor)
    return jnp.sum(jnp.where(diagonal((count, LANES)), row, 0.0), axis=1, keepdims=True)


def event_kernel(place_ref, local_ref, parts_ref, events_ref, first_ref, second_ref, total_ref):
    local = local_ref[...]
    endpoints, length = local.shape
    risk = log_sum(local, carried_later(place_ref[0], parts_ref))
    happened = events_ref[...] == 1
    peak = jnp.where(happened, -risk, log_floor)
    first = happened.astype(f32)
    second = first
    for step in steps(length):
        far_peak = behind(peak, step, log_floor)
        far_first = behind(first, step, 0.0)
        far_second = behind(second, step, 0.0)
        gap = peak - far_peak
        shrink = jnp.exp(-jnp.abs(gap))
        near = gap >= 0
        square = shrink * shrink
        first = jnp.where(near, first + far_first * shrink, first * shrink + far_first)
        second = jnp.where(near, second + far_second * square, second * square + far_second)
        peak = jnp.maximum(peak, far_peak)
    some = first > 0
    first_log = jnp.where(some, peak + jnp.log(first), log_floor)
    second_log = jnp.where(some, 2.0 * peak + jnp.log(second), log_floor)
    end = length - 1
    share_row(jnp.concatenate([first_log[:, end:], second_log[:, end:]], axis=0), total_ref)
    first_ref[...] = first_log
    second_ref[...] = second_log


def close_kernel(first_ref, second_ref, tie_ref, first_out, second_out):
    first = first_ref[...]
    second = second_ref[...]
    tie = tie_rows(tie_ref, first)
    length = first.shape[1]
    lane = lax.broadcasted_iota(jnp.int32, first.shape, 1)
    closes = (lane == length - 1) | (tie != pltpu.roll(tie, length - 1, 1))
    first = jnp.where(closes, first, -log_floor)
    second = jnp.where(closes, second, -log_floor)
    for step in steps(length):
        first = jnp.minimum(first, ahead(first, step, -log_floor))
        second = jnp.minimum(second, ahead(second, step, -log_floor))
    first_out[...] = first
    second_out[...] = second


def grad_kernel(place_ref, margins_ref, events_ref, node_ref, first_ref, second_ref, parts_ref, grad_ref, hess_ref, pair_ref):
    margins = margins_ref[...]
    endpoints = margins.shape[0]
    carry = carried_earlier(place_ref[0], parts_ref, 2 * endpoints)
    first_log = log_sum(first_ref[...], carry[0:endpoints])
    second_log = log_sum(second_ref[...], carry[endpoints:])
    first = jnp.exp(margins + first_log)
    second = jnp.exp(2.0 * margins + second_log)
    grad = first - (events_ref[...] == 1).astype(f32)
    hess = first - second
    grad_ref[...] = grad.astype(bf16)
    hess_ref[...] = hess.astype(bf16)
    chosen = tie_rows(node_ref, margins) == 1
    pair_ref[0:endpoints] = jnp.where(chosen, grad, 0.0).astype(bf16)
    pair_ref[endpoints:] = jnp.where(chosen, hess, 0.0).astype(bf16)


def add_block(codes, pairs, sums_ref, feature_count, finish=None):
    length = pairs.shape[1]
    level = lax.broadcasted_iota(jnp.int32, (HALF, length), 0).astype(bf16)
    nothing = jnp.zeros_like(pairs)
    upper = codes >= bf16(HALF)
    low = jnp.where(upper, codes - bf16(HALF), codes)
    high = jnp.where(upper, bf16(1), bf16(0))
    for f in range(feature_count):
        up = jnp.broadcast_to(high[f : f + 1], pairs.shape) == bf16(1)
        left = jnp.concatenate([jnp.where(up, nothing, pairs), jnp.where(up, pairs, nothing)], axis=0)
        reach = jnp.where(level >= low[f : f + 1], bf16(1), bf16(0))
        sums = sums_ref[f] + lax.dot_general(left, reach, NT, preferred_element_type=f32)
        if finish is None:
            sums_ref[f] = sums
        else:
            finish(f, sums)


def write_gain(gain_ref, f, sums):
    channels = sums.shape[0] // 2
    quarter = channels // 4

    def part(x):
        grad = jnp.concatenate([x[0:quarter], x[2 * quarter : 3 * quarter]], axis=0)
        hess = jnp.concatenate([x[quarter : 2 * quarter], x[3 * quarter :]], axis=0)
        return grad * grad / (hess + 1.0)

    lower = sums[0:channels]
    uppers = sums[channels:] + lower[:, HALF - 1 :]
    whole = uppers[:, HALF - 1 :]
    whole_part = part(whole)
    for side, left in enumerate((lower, uppers)):
        value = part(left) + part(whole - left) - whole_part
        gain_ref[f : f + 1, side * HALF : (side + 1) * HALF] = jnp.mean(value, axis=0, keepdims=True)


def hist_kernel(blocks, feature_count, first, last, *refs):
    if first:
        codes_ref, mine_ref, other_ref, *outs = refs
    else:
        codes_ref, mine_ref, other_ref, before_ref, *outs = refs
    sums_ref = outs[-1]
    block = pl.program_id(0)

    @pl.when(block == 0)
    def _():
        sums_ref[...] = jnp.zeros_like(sums_ref) if first else before_ref[...]

    pairs = jnp.concatenate([mine_ref[0], other_ref[0]], axis=0)
    if not last:
        add_block(codes_ref[0], pairs, sums_ref, feature_count)
        return

    @pl.when(block < blocks - 1)
    def _():
        add_block(codes_ref[0], pairs, sums_ref, feature_count)

    @pl.when(block == blocks - 1)
    def _():
        add_block(codes_ref[0], pairs, sums_ref, feature_count, functools.partial(write_gain, outs[0]))


def histogram(codes, mine, other, before, last):
    blocks, feature_count, length = codes.shape
    half = mine.shape[1]
    sums = (feature_count, 4 * half, HALF)
    operands = [codes, mine, other]
    in_specs = [
        pl.BlockSpec((1, feature_count, length), lambda i: (i, 0, 0)),
        pl.BlockSpec((1, half, length), lambda i: (i, 0, 0)),
        pl.BlockSpec((1, half, length), lambda i: (i, 0, 0)),
    ]
    whole = pl.BlockSpec(sums, lambda i: (0, 0, 0))
    if before is not None:
        operands.append(before)
        in_specs.append(whole)
    return pl.pallas_call(
        functools.partial(hist_kernel, blocks, feature_count, before is None, last),
        out_shape=shape(feature_count, BINS) if last else shape(*sums),
        grid=(blocks,),
        in_specs=in_specs,
        out_specs=pl.BlockSpec((feature_count, BINS), lambda i: (0, 0)) if last else whole,
        scratch_shapes=[pltpu.VMEM(sums, f32)] if last else [],
        input_output_aliases={3: 0} if before is not None and not last else {},
        name="hist",
        compiler_params=pltpu.CompilerParams(dimension_semantics=("arbitrary",), vmem_limit_bytes=20 << 20),
        cost_estimate=pl.CostEstimate(
            flops=blocks * feature_count * 2 * (4 * half) * HALF * length * 4,
            bytes_accessed=blocks * (feature_count + 2 * half) * length * 2,
            transcendentals=0,
        ),
    )(*operands)


def call(kernel, out_shape, name, *operands, place=False):
    single = isinstance(out_shape, jax.ShapeDtypeStruct)
    return pl.pallas_call(
        kernel,
        out_shape=out_shape,
        in_specs=([SMEM] if place else []) + [VMEM] * (len(operands) - place),
        out_specs=VMEM if single else (VMEM,) * len(out_shape),
        name=name,
        compiler_params=pltpu.CompilerParams(vmem_limit_bytes=12 << 20),
    )(*operands)


def shape(*dims, dtype=f32):
    return jax.ShapeDtypeStruct(dims, dtype)


VMEM = pl.BlockSpec(memory_space=pltpu.VMEM)
SMEM = pl.BlockSpec(memory_space=pltpu.SMEM)


def ring(devices, d):
    return [(i, (i + 4 * d) % devices) for i in range(devices)]


def flip(devices, d):
    return [(i, i ^ d) for i in range(devices)]


def swap(x):
    return lax.ppermute(x, "feat", [(0, 1), (1, 0)])


def pick(x, index, axis):
    return lax.dynamic_index_in_dim(x, index, axis, False)


def send_planes(codes, devices):
    planes = devices // 4
    plane = lax.axis_index("tm") // 4
    codes = codes.reshape(planes, 4, -1, codes.shape[1])
    held = [pick(codes, plane, 0)]
    for d in range(1, planes):
        held.append(lax.ppermute(pick(codes, (plane + d) % planes, 0), "tm", ring(devices, d)))
    return held


def spread(held, plane, pairs, devices):
    planes = devices // 4
    here = lax.axis_index("tm") % 4
    column = [lax.ppermute(pairs, "tm", ring(devices, d)) for d in range(1, planes)]
    beside = [lax.ppermute(pairs, "tm", flip(devices, d)) for d in range(1, 3)]
    own = pick(held[0], here, 0)
    near = jnp.stack([pick(h, here, 0) for h in held[1:]])
    far = [
        lax.ppermute(jnp.stack([pick(h, here ^ d, 0) for h in (held if d == 3 else held[1:])]), "tm", flip(devices, d))
        for d in range(1, 4)
    ]
    *column, pairs = lax.optimization_barrier((*column, pairs))
    column_sent = jnp.stack(column)
    there = [lax.ppermute(column_sent, "tm", flip(devices, d)) for d in range(1, 3)]
    there.append(lax.ppermute(jnp.stack([pairs] + column), "tm", flip(devices, 3)))
    column = column_sent
    other = swap(column)
    beside = jnp.stack([pairs] + beside)
    sums = histogram(jnp.stack([own] + plane), beside, swap(beside), None, False)
    cut = planes - 2
    sums = histogram(near[:cut], column[:cut], other[:cut], sums, False)
    there[0], sums = lax.optimization_barrier((there[0], sums))
    back = [swap(x) for x in there]
    sums = histogram(near[cut:], column[cut:], other[cut:], sums, False)
    for d in range(1, 4):
        sums = histogram(far[d - 1], there[d - 1], back[d - 1], sums, d == 3)
    return sums


def spread_any(codes, pairs):
    rows = lax.all_gather(pairs, "tm")
    return histogram(codes, rows, swap(rows), None, True)


def on_device(devices, margins, events, tie_group, in_node, bins):
    endpoints, length = margins.shape
    here = lax.axis_index("tm")[None].astype(jnp.int32)
    mine = bins.shape[0] // devices
    rows = shape(endpoints, length)
    narrow = shape(endpoints, length, dtype=bf16)

    def exchange(total):
        return lax.all_to_all(total, "tm", 0, 0)

    risk, total = call(risk_kernel, (rows, shape(devices, endpoints, LANES)), "risk", margins)
    parts = exchange(total)
    local = call(open_kernel, rows, "opens", risk, tie_group)
    bins, local = lax.optimization_barrier((bins, local))
    codes = bins.astype(bf16)
    blocked = devices == 16
    if blocked:
        codes = send_planes(codes, devices)
    else:
        codes = lax.all_to_all(codes.reshape(devices, mine, length), "tm", 0, 0)
    first, second, total = call(
        event_kernel, (rows, rows, shape(devices, 1, LANES)), "events",
        here, local, parts, events, place=True,
    )
    parts = exchange(total)
    if blocked:
        column = lax.axis_index("tm") % 4
        aside, second = lax.optimization_barrier((codes[0], second))
        plane = [lax.ppermute(pick(aside, column ^ d, 0), "tm", flip(devices, d)) for d in range(1, 3)]
    first, second = call(close_kernel, (rows, rows), "closes", first, second, tie_group)
    codes, parts = lax.optimization_barrier((codes, parts))
    grad, hess, pairs = call(
        grad_kernel, (narrow, narrow, shape(2 * endpoints, length, dtype=bf16)), "grads",
        here, margins, events, in_node, first, second, parts, place=True,
    )
    if blocked:
        plane, pairs = lax.optimization_barrier((plane, pairs))
    gain = spread(codes, plane, pairs, devices) if blocked else spread_any(codes, pairs)
    return (grad, hess, gain[None])


def solution(mesh):
    in_specs = (P("feat", "tm"), P("feat", "tm"), P("tm"), P("tm"), P("feat", "tm"))
    out_specs = (P("feat", "tm"), P("feat", "tm"), P("feat", "tm", None))
    return jax.shard_map(
        functools.partial(on_device, mesh.shape["tm"]),
        mesh=mesh, in_specs=in_specs, out_specs=out_specs, check_vma=False,
    )
```

```python
import functools

import jax
import jax.numpy as jnp
from jax import lax
from jax.experimental import pallas as pl
from jax.experimental.pallas import tpu as pltpu
from jax.sharding import PartitionSpec as P

BINS = 256
HALF = BINS // 2
LANES = 128
log_floor = -1e30
NT = (((1,), (1,)), ((), ()))
f32 = jnp.float32
bf16 = jnp.bfloat16


def ahead(x, step, fill):
    length = x.shape[1]
    pad = jnp.full((x.shape[0], step), fill, x.dtype)
    if step % LANES == 0:
        return jnp.concatenate([x[:, step:], pad], axis=1)
    lane = lax.broadcasted_iota(jnp.int32, x.shape, 1)
    return jnp.where(lane < length - step, pltpu.roll(x, length - step, 1), fill)


def behind(x, step, fill):
    length = x.shape[1]
    pad = jnp.full((x.shape[0], step), fill, x.dtype)
    if step % LANES == 0:
        return jnp.concatenate([pad, x[:, : length - step]], axis=1)
    lane = lax.broadcasted_iota(jnp.int32, x.shape, 1)
    return jnp.where(lane >= step, pltpu.roll(x, step, 1), fill)


def steps(length):
    step = 1
    while step < length:
        yield step
        step *= 2


def log_sum(a, b):
    peak = jnp.maximum(a, b)
    return peak + jnp.log(1.0 + jnp.exp(-jnp.abs(a - b)))


def share(total, total_ref):
    wide = jnp.broadcast_to(total, total_ref.shape[1:])
    for k in range(total_ref.shape[0]):
        total_ref[k] = wide


def share_row(total, total_ref):
    row = jnp.sum(jnp.where(diagonal((total.shape[0], LANES)), total, 0.0), axis=0, keepdims=True)
    for k in range(total_ref.shape[0]):
        total_ref[k] = row


def diagonal(like):
    return lax.broadcasted_iota(jnp.int32, like, 0) == lax.broadcasted_iota(jnp.int32, like, 1)


def risk_kernel(margins_ref, risk_ref, total_ref):
    peak = margins_ref[...]
    length = peak.shape[1]
    mass = jnp.ones_like(peak)
    for step in steps(length):
        far_peak = ahead(peak, step, log_floor)
        far_mass = ahead(mass, step, 0.0)
        gap = peak - far_peak
        shrink = jnp.exp(-jnp.abs(gap))
        mass = jnp.where(gap >= 0, mass + far_mass * shrink, mass * shrink + far_mass)
        peak = jnp.maximum(peak, far_peak)
    risk = peak + jnp.log(mass)
    share(risk[:, 0:1], total_ref)
    risk_ref[...] = risk


def tie_rows(tie_ref, like):
    return jnp.broadcast_to(tie_ref[...][None], like.shape)


def open_kernel(risk_ref, tie_ref, local_ref):
    risk = risk_ref[...]
    tie = tie_rows(tie_ref, risk)
    lane = lax.broadcasted_iota(jnp.int32, risk.shape, 1)
    opens = (lane == 0) | (tie != pltpu.roll(tie, 1, 1))
    filled = jnp.where(opens, risk, -log_floor)
    for step in steps(risk.shape[1]):
        filled = jnp.minimum(filled, behind(filled, step, -log_floor))
    local_ref[...] = filled


def carried_later(place, parts_ref):
    held = [jnp.where(place < k, parts_ref[k], log_floor) for k in range(parts_ref.shape[0])]
    peak = functools.reduce(jnp.maximum, held)
    mass = functools.reduce(jnp.add, [jnp.exp(h - peak) for h in held])
    return jnp.where(peak > 0.5 * log_floor, peak + jnp.log(mass), log_floor)[:, 0:1]


def carried_earlier(place, parts_ref, count):
    parts = jnp.concatenate([parts_ref[k] for k in range(parts_ref.shape[0])], axis=0)
    device = lax.broadcasted_iota(jnp.int32, parts.shape, 0)
    held = jnp.where(device < place, parts, log_floor)
    peak = jnp.max(held, axis=0, keepdims=True)
    mass = jnp.sum(jnp.exp(held - peak), axis=0, keepdims=True)
    row = jnp.where(peak > 0.5 * log_floor, peak + jnp.log(mass), log_floor)
    return jnp.sum(jnp.where(diagonal((count, LANES)), row, 0.0), axis=1, keepdims=True)


def event_kernel(place_ref, local_ref, parts_ref, events_ref, first_ref, second_ref, total_ref):
    local = local_ref[...]
    endpoints, length = local.shape
    risk = log_sum(local, carried_later(place_ref[0], parts_ref))
    happened = events_ref[...] == 1
    peak = jnp.where(happened, -risk, log_floor)
    first = happened.astype(f32)
    second = first
    for step in steps(length):
        far_peak = behind(peak, step, log_floor)
        far_first = behind(first, step, 0.0)
        far_second = behind(second, step, 0.0)
        gap = peak - far_peak
        shrink = jnp.exp(-jnp.abs(gap))
        near = gap >= 0
        square = shrink * shrink
        first = jnp.where(near, first + far_first * shrink, first * shrink + far_first)
        second = jnp.where(near, second + far_second * square, second * square + far_second)
        peak = jnp.maximum(peak, far_peak)
    some = first > 0
    first_log = jnp.where(some, peak + jnp.log(first), log_floor)
    second_log = jnp.where(some, 2.0 * peak + jnp.log(second), log_floor)
    end = length - 1
    share_row(jnp.concatenate([first_log[:, end:], second_log[:, end:]], axis=0), total_ref)
    first_ref[...] = first_log
    second_ref[...] = second_log


def close_kernel(first_ref, second_ref, tie_ref, first_out, second_out):
    first = first_ref[...]
    second = second_ref[...]
    tie = tie_rows(tie_ref, first)
    length = first.shape[1]
    lane = lax.broadcasted_iota(jnp.int32, first.shape, 1)
    closes = (lane == length - 1) | (tie != pltpu.roll(tie, length - 1, 1))
    first = jnp.where(closes, first, -log_floor)
    second = jnp.where(closes, second, -log_floor)
    for step in steps(length):
        first = jnp.minimum(first, ahead(first, step, -log_floor))
        second = jnp.minimum(second, ahead(second, step, -log_floor))
    first_out[...] = first
    second_out[...] = second


def grad_kernel(place_ref, margins_ref, events_ref, node_ref, first_ref, second_ref, parts_ref, grad_ref, hess_ref, pair_ref):
    margins = margins_ref[...]
    endpoints = margins.shape[0]
    carry = carried_earlier(place_ref[0], parts_ref, 2 * endpoints)
    first_log = log_sum(first_ref[...], carry[0:endpoints])
    second_log = log_sum(second_ref[...], carry[endpoints:])
    first = jnp.exp(margins + first_log)
    second = jnp.exp(2.0 * margins + second_log)
    grad = first - (events_ref[...] == 1).astype(f32)
    hess = first - second
    grad_ref[...] = grad.astype(bf16)
    hess_ref[...] = hess.astype(bf16)
    chosen = tie_rows(node_ref, margins) == 1
    pair_ref[0:endpoints] = jnp.where(chosen, grad, 0.0).astype(bf16)
    pair_ref[endpoints:] = jnp.where(chosen, hess, 0.0).astype(bf16)


def add_block(codes, pairs, sums_ref, feature_count, finish=None):
    length = pairs.shape[1]
    level = lax.broadcasted_iota(jnp.int32, (HALF, length), 0).astype(bf16)
    nothing = jnp.zeros_like(pairs)
    upper = codes >= bf16(HALF)
    low = jnp.where(upper, codes - bf16(HALF), codes)
    high = jnp.where(upper, bf16(1), bf16(0))
    for f in range(feature_count):
        up = jnp.broadcast_to(high[f : f + 1], pairs.shape) == bf16(1)
        left = jnp.concatenate([jnp.where(up, nothing, pairs), jnp.where(up, pairs, nothing)], axis=0)
        reach = jnp.where(level >= low[f : f + 1], bf16(1), bf16(0))
        sums = sums_ref[f] + lax.dot_general(left, reach, NT, preferred_element_type=f32)
        if finish is None:
            sums_ref[f] = sums
        else:
            finish(f, sums)


def write_gain(gain_ref, f, sums):
    channels = sums.shape[0] // 2
    quarter = channels // 4

    def part(x):
        grad = jnp.concatenate([x[0:quarter], x[2 * quarter : 3 * quarter]], axis=0)
        hess = jnp.concatenate([x[quarter : 2 * quarter], x[3 * quarter :]], axis=0)
        return grad * grad / (hess + 1.0)

    lower = sums[0:channels]
    uppers = sums[channels:] + lower[:, HALF - 1 :]
    whole = uppers[:, HALF - 1 :]
    whole_part = part(whole)
    for side, left in enumerate((lower, uppers)):
        value = part(left) + part(whole - left) - whole_part
        gain_ref[f : f + 1, side * HALF : (side + 1) * HALF] = jnp.mean(value, axis=0, keepdims=True)


def hist_kernel(steps, feature_count, first, last, *refs):
    if first:
        codes_ref, mine_ref, other_ref, *outs = refs
    else:
        codes_ref, mine_ref, other_ref, before_ref, *outs = refs
    sums_ref = outs[-1]
    step = pl.program_id(0)
    blocks = codes_ref.shape[0]

    @pl.when(step == 0)
    def _():
        sums_ref[...] = jnp.zeros_like(sums_ref) if first else before_ref[...]

    codes = jnp.concatenate([codes_ref[k] for k in range(blocks)], axis=1)
    mine = jnp.concatenate([mine_ref[k] for k in range(blocks)], axis=1)
    other = jnp.concatenate([other_ref[k] for k in range(blocks)], axis=1)
    pairs = jnp.concatenate([mine, other], axis=0)
    if not last:
        add_block(codes, pairs, sums_ref, feature_count)
        return
    finish = functools.partial(write_gain, outs[0])
    if steps == 1:
        add_block(codes, pairs, sums_ref, feature_count, finish)
        return

    @pl.when(step < steps - 1)
    def _():
        add_block(codes, pairs, sums_ref, feature_count)

    @pl.when(step == steps - 1)
    def _():
        add_block(codes, pairs, sums_ref, feature_count, finish)


def histogram(codes, mine, other, before, last):
    blocks, feature_count, length = codes.shape
    half = mine.shape[1]
    joined = next(n for n in (3, 2, 1) if blocks % n == 0)
    sums = (feature_count, 4 * half, HALF)
    operands = [codes, mine, other]
    in_specs = [
        pl.BlockSpec((joined, feature_count, length), lambda i: (i, 0, 0)),
        pl.BlockSpec((joined, half, length), lambda i: (i, 0, 0)),
        pl.BlockSpec((joined, half, length), lambda i: (i, 0, 0)),
    ]
    whole = pl.BlockSpec(sums, lambda i: (0, 0, 0))
    if before is not None:
        operands.append(before)
        in_specs.append(whole)
    return pl.pallas_call(
        functools.partial(hist_kernel, blocks // joined, feature_count, before is None, last),
        out_shape=shape(feature_count, BINS) if last else shape(*sums),
        grid=(blocks // joined,),
        in_specs=in_specs,
        out_specs=pl.BlockSpec((feature_count, BINS), lambda i: (0, 0)) if last else whole,
        scratch_shapes=[pltpu.VMEM(sums, f32)] if last else [],
        input_output_aliases={3: 0} if before is not None and not last else {},
        name="hist",
        compiler_params=pltpu.CompilerParams(dimension_semantics=("arbitrary",), vmem_limit_bytes=20 << 20),
        cost_estimate=pl.CostEstimate(
            flops=blocks * feature_count * 2 * (4 * half) * HALF * length * 4,
            bytes_accessed=blocks * (feature_count + 2 * half) * length * 2,
            transcendentals=0,
        ),
    )(*operands)


def call(kernel, out_shape, name, *operands, place=False):
    single = isinstance(out_shape, jax.ShapeDtypeStruct)
    return pl.pallas_call(
        kernel,
        out_shape=out_shape,
        in_specs=([SMEM] if place else []) + [VMEM] * (len(operands) - place),
        out_specs=VMEM if single else (VMEM,) * len(out_shape),
        name=name,
        compiler_params=pltpu.CompilerParams(vmem_limit_bytes=12 << 20),
    )(*operands)


def shape(*dims, dtype=f32):
    return jax.ShapeDtypeStruct(dims, dtype)


VMEM = pl.BlockSpec(memory_space=pltpu.VMEM)
SMEM = pl.BlockSpec(memory_space=pltpu.SMEM)


def ring(devices, d):
    return [(i, (i + 4 * d) % devices) for i in range(devices)]


def flip(devices, d):
    return [(i, i ^ d) for i in range(devices)]


def swap(x):
    return lax.ppermute(x, "feat", [(0, 1), (1, 0)])


def pick(x, index, axis):
    return lax.dynamic_index_in_dim(x, index, axis, False)


def send_planes(codes, devices):
    planes = devices // 4
    plane = lax.axis_index("tm") // 4
    codes = codes.reshape(planes, 4, -1, codes.shape[1])
    held = [pick(codes, plane, 0)]
    for d in range(1, planes):
        held.append(lax.ppermute(pick(codes, (plane + d) % planes, 0), "tm", ring(devices, d)))
    return held


def spread(held, plane, pairs, devices):
    planes = devices // 4
    here = lax.axis_index("tm") % 4
    column = [lax.ppermute(pairs, "tm", ring(devices, d)) for d in range(1, planes)]
    beside = [lax.ppermute(pairs, "tm", flip(devices, d)) for d in range(1, 4)]
    own = pick(held[0], here, 0)
    near = jnp.stack([pick(h, here, 0) for h in held[1:]])
    far = [
        lax.ppermute(jnp.stack([pick(h, here ^ d, 0) for h in held[1:]]), "tm", flip(devices, d))
        for d in range(1, 4)
    ]
    *column, pairs = lax.optimization_barrier((*column, pairs))
    column = jnp.stack(column)
    there = [lax.ppermute(column, "tm", flip(devices, d)) for d in range(1, 4)]
    other = swap(column)
    beside = jnp.stack([pairs] + beside)
    sums = histogram(jnp.stack([own] + plane), beside, swap(beside), None, False)
    cut = planes - 2
    sums = histogram(near[:cut], column[:cut], other[:cut], sums, False)
    there[0], sums = lax.optimization_barrier((there[0], sums))
    back = [swap(x) for x in there]
    sums = histogram(near[cut:], column[cut:], other[cut:], sums, False)
    for d in range(1, 4):
        sums = histogram(far[d - 1], there[d - 1], back[d - 1], sums, d == 3)
    return sums


def spread_any(codes, pairs):
    rows = lax.all_gather(pairs, "tm")
    return histogram(codes, rows, swap(rows), None, True)


def on_device(devices, margins, events, tie_group, in_node, bins):
    endpoints, length = margins.shape
    here = lax.axis_index("tm")[None].astype(jnp.int32)
    mine = bins.shape[0] // devices
    rows = shape(endpoints, length)
    narrow = shape(endpoints, length, dtype=bf16)

    def exchange(total):
        return lax.all_to_all(total, "tm", 0, 0)

    risk, total = call(risk_kernel, (rows, shape(devices, endpoints, LANES)), "risk", margins)
    parts = exchange(total)
    local = call(open_kernel, rows, "opens", risk, tie_group)
    bins, local = lax.optimization_barrier((bins, local))
    codes = bins.astype(bf16)
    blocked = devices == 16
    if blocked:
        codes = send_planes(codes, devices)
    else:
        codes = lax.all_to_all(codes.reshape(devices, mine, length), "tm", 0, 0)
    first, second, total = call(
        event_kernel, (rows, rows, shape(devices, 1, LANES)), "events",
        here, local, parts, events, place=True,
    )
    parts = exchange(total)
    if blocked:
        column = lax.axis_index("tm") % 4
        aside, second = lax.optimization_barrier((codes[0], second))
        plane = [lax.ppermute(pick(aside, column ^ d, 0), "tm", flip(devices, d)) for d in range(1, 4)]
    first, second = call(close_kernel, (rows, rows), "closes", first, second, tie_group)
    codes, parts = lax.optimization_barrier((codes, parts))
    grad, hess, pairs = call(
        grad_kernel, (narrow, narrow, shape(2 * endpoints, length, dtype=bf16)), "grads",
        here, margins, events, in_node, first, second, parts, place=True,
    )
    if blocked:
        plane, pairs = lax.optimization_barrier((plane, pairs))
    gain = spread(codes, plane, pairs, devices) if blocked else spread_any(codes, pairs)
    return (grad, hess, gain[None])


def solution(mesh):
    in_specs = (P("feat", "tm"), P("feat", "tm"), P("tm"), P("tm"), P("feat", "tm"))
    out_specs = (P("feat", "tm"), P("feat", "tm"), P("feat", "tm", None))
    return jax.shard_map(
        functools.partial(on_device, mesh.shape["tm"]),
        mesh=mesh, in_specs=in_specs, out_specs=out_specs, check_vma=False,
    )
```

```python
import functools

import jax
import jax.numpy as jnp
from jax import lax
from jax.experimental import pallas as pl
from jax.experimental.pallas import tpu as pltpu
from jax.sharding import PartitionSpec as P

BINS = 256
HALF = BINS // 2
LANES = 128
log_floor = -1e30
NT = (((1,), (1,)), ((), ()))
f32 = jnp.float32
bf16 = jnp.bfloat16


def ahead(x, step, fill):
    length = x.shape[1]
    pad = jnp.full((x.shape[0], step), fill, x.dtype)
    if step % LANES == 0:
        return jnp.concatenate([x[:, step:], pad], axis=1)
    lane = lax.broadcasted_iota(jnp.int32, x.shape, 1)
    return jnp.where(lane < length - step, pltpu.roll(x, length - step, 1), fill)


def behind(x, step, fill):
    length = x.shape[1]
    pad = jnp.full((x.shape[0], step), fill, x.dtype)
    if step % LANES == 0:
        return jnp.concatenate([pad, x[:, : length - step]], axis=1)
    lane = lax.broadcasted_iota(jnp.int32, x.shape, 1)
    return jnp.where(lane >= step, pltpu.roll(x, step, 1), fill)


def steps(length):
    step = 1
    while step < length:
        yield step
        step *= 2


def log_sum(a, b):
    peak = jnp.maximum(a, b)
    return peak + jnp.log(1.0 + jnp.exp(-jnp.abs(a - b)))


def share(total, total_ref):
    wide = jnp.broadcast_to(total, total_ref.shape[1:])
    for k in range(total_ref.shape[0]):
        total_ref[k] = wide


def share_row(total, total_ref):
    row = jnp.sum(jnp.where(diagonal((total.shape[0], LANES)), total, 0.0), axis=0, keepdims=True)
    for k in range(total_ref.shape[0]):
        total_ref[k] = row


def diagonal(like):
    return lax.broadcasted_iota(jnp.int32, like, 0) == lax.broadcasted_iota(jnp.int32, like, 1)


def risk_kernel(margins_ref, risk_ref, total_ref):
    peak = margins_ref[...]
    length = peak.shape[1]
    mass = jnp.ones_like(peak)
    for step in steps(length):
        far_peak = ahead(peak, step, log_floor)
        far_mass = ahead(mass, step, 0.0)
        gap = peak - far_peak
        shrink = jnp.exp(-jnp.abs(gap))
        mass = jnp.where(gap >= 0, mass + far_mass * shrink, mass * shrink + far_mass)
        peak = jnp.maximum(peak, far_peak)
    risk = peak + jnp.log(mass)
    share(risk[:, 0:1], total_ref)
    risk_ref[...] = risk


def tie_rows(tie_ref, like):
    return jnp.broadcast_to(tie_ref[...][None], like.shape)


def open_kernel(risk_ref, tie_ref, local_ref):
    risk = risk_ref[...]
    tie = tie_rows(tie_ref, risk)
    lane = lax.broadcasted_iota(jnp.int32, risk.shape, 1)
    opens = (lane == 0) | (tie != pltpu.roll(tie, 1, 1))
    filled = jnp.where(opens, risk, -log_floor)
    for step in steps(risk.shape[1]):
        filled = jnp.minimum(filled, behind(filled, step, -log_floor))
    local_ref[...] = filled


def carried_later(place, parts_ref):
    held = [jnp.where(place < k, parts_ref[k], log_floor) for k in range(parts_ref.shape[0])]
    peak = functools.reduce(jnp.maximum, held)
    mass = functools.reduce(jnp.add, [jnp.exp(h - peak) for h in held])
    return jnp.where(peak > 0.5 * log_floor, peak + jnp.log(mass), log_floor)[:, 0:1]


def carried_earlier(place, parts_ref, count):
    parts = jnp.concatenate([parts_ref[k] for k in range(parts_ref.shape[0])], axis=0)
    device = lax.broadcasted_iota(jnp.int32, parts.shape, 0)
    held = jnp.where(device < place, parts, log_floor)
    peak = jnp.max(held, axis=0, keepdims=True)
    mass = jnp.sum(jnp.exp(held - peak), axis=0, keepdims=True)
    row = jnp.where(peak > 0.5 * log_floor, peak + jnp.log(mass), log_floor)
    return jnp.sum(jnp.where(diagonal((count, LANES)), row, 0.0), axis=1, keepdims=True)


def event_kernel(place_ref, local_ref, parts_ref, events_ref, first_ref, second_ref, total_ref):
    local = local_ref[...]
    endpoints, length = local.shape
    risk = log_sum(local, carried_later(place_ref[0], parts_ref))
    happened = events_ref[...] == 1
    peak = jnp.where(happened, -risk, log_floor)
    first = happened.astype(f32)
    second = first
    for step in steps(length):
        far_peak = behind(peak, step, log_floor)
        far_first = behind(first, step, 0.0)
        far_second = behind(second, step, 0.0)
        gap = peak - far_peak
        shrink = jnp.exp(-jnp.abs(gap))
        near = gap >= 0
        square = shrink * shrink
        first = jnp.where(near, first + far_first * shrink, first * shrink + far_first)
        second = jnp.where(near, second + far_second * square, second * square + far_second)
        peak = jnp.maximum(peak, far_peak)
    some = first > 0
    first_log = jnp.where(some, peak + jnp.log(first), log_floor)
    second_log = jnp.where(some, 2.0 * peak + jnp.log(second), log_floor)
    end = length - 1
    share_row(jnp.concatenate([first_log[:, end:], second_log[:, end:]], axis=0), total_ref)
    first_ref[...] = first_log
    second_ref[...] = second_log


def close_kernel(first_ref, second_ref, tie_ref, first_out, second_out):
    first = first_ref[...]
    second = second_ref[...]
    tie = tie_rows(tie_ref, first)
    length = first.shape[1]
    lane = lax.broadcasted_iota(jnp.int32, first.shape, 1)
    closes = (lane == length - 1) | (tie != pltpu.roll(tie, length - 1, 1))
    first = jnp.where(closes, first, -log_floor)
    second = jnp.where(closes, second, -log_floor)
    for step in steps(length):
        first = jnp.minimum(first, ahead(first, step, -log_floor))
        second = jnp.minimum(second, ahead(second, step, -log_floor))
    first_out[...] = first
    second_out[...] = second


def grad_kernel(place_ref, margins_ref, events_ref, node_ref, first_ref, second_ref, parts_ref, grad_ref, hess_ref, pair_ref):
    margins = margins_ref[...]
    endpoints = margins.shape[0]
    carry = carried_earlier(place_ref[0], parts_ref, 2 * endpoints)
    first_log = log_sum(first_ref[...], carry[0:endpoints])
    second_log = log_sum(second_ref[...], carry[endpoints:])
    first = jnp.exp(margins + first_log)
    second = jnp.exp(2.0 * margins + second_log)
    grad = first - (events_ref[...] == 1).astype(f32)
    hess = first - second
    grad_ref[...] = grad.astype(bf16)
    hess_ref[...] = hess.astype(bf16)
    chosen = tie_rows(node_ref, margins) == 1
    pair_ref[0:endpoints] = jnp.where(chosen, grad, 0.0).astype(bf16)
    pair_ref[endpoints:] = jnp.where(chosen, hess, 0.0).astype(bf16)


def add_block(codes, pairs, sums_ref, feature_count, finish=None):
    length = pairs.shape[1]
    level = lax.broadcasted_iota(jnp.int32, (HALF, length), 0).astype(bf16)
    nothing = jnp.zeros_like(pairs)
    upper = codes >= bf16(HALF)
    low = jnp.where(upper, codes - bf16(HALF), codes)
    high = jnp.where(upper, bf16(1), bf16(0))
    for f in range(feature_count):
        up = jnp.broadcast_to(high[f : f + 1], pairs.shape) == bf16(1)
        left = jnp.concatenate([jnp.where(up, nothing, pairs), jnp.where(up, pairs, nothing)], axis=0)
        reach = jnp.where(level >= low[f : f + 1], bf16(1), bf16(0))
        sums = sums_ref[f] + lax.dot_general(left, reach, NT, preferred_element_type=f32)
        if finish is None:
            sums_ref[f] = sums
        else:
            finish(f, sums)


def write_gain(gain_ref, f, sums):
    channels = sums.shape[0] // 2
    quarter = channels // 4

    def part(x):
        grad = jnp.concatenate([x[0:quarter], x[2 * quarter : 3 * quarter]], axis=0)
        hess = jnp.concatenate([x[quarter : 2 * quarter], x[3 * quarter :]], axis=0)
        return grad * grad / (hess + 1.0)

    lower = sums[0:channels]
    uppers = sums[channels:] + lower[:, HALF - 1 :]
    whole = uppers[:, HALF - 1 :]
    whole_part = part(whole)
    for side, left in enumerate((lower, uppers)):
        value = part(left) + part(whole - left) - whole_part
        gain_ref[f : f + 1, side * HALF : (side + 1) * HALF] = jnp.mean(value, axis=0, keepdims=True)


def hist_kernel(steps, feature_count, first, last, *refs):
    if first:
        codes_ref, mine_ref, other_ref, *outs = refs
    else:
        codes_ref, mine_ref, other_ref, before_ref, *outs = refs
    sums_ref = outs[-1]
    step = pl.program_id(0)
    blocks = codes_ref.shape[0]

    @pl.when(step == 0)
    def _():
        sums_ref[...] = jnp.zeros_like(sums_ref) if first else before_ref[...]

    codes = jnp.concatenate([codes_ref[k] for k in range(blocks)], axis=1)
    mine = jnp.concatenate([mine_ref[k] for k in range(blocks)], axis=1)
    other = jnp.concatenate([other_ref[k] for k in range(blocks)], axis=1)
    pairs = jnp.concatenate([mine, other], axis=0)
    if not last:
        add_block(codes, pairs, sums_ref, feature_count)
        return
    finish = functools.partial(write_gain, outs[0])
    if steps == 1:
        add_block(codes, pairs, sums_ref, feature_count, finish)
        return

    @pl.when(step < steps - 1)
    def _():
        add_block(codes, pairs, sums_ref, feature_count)

    @pl.when(step == steps - 1)
    def _():
        add_block(codes, pairs, sums_ref, feature_count, finish)


def histogram(codes, mine, other, before, last):
    blocks, feature_count, length = codes.shape
    half = mine.shape[1]
    joined = next(n for n in (3, 2, 1) if blocks % n == 0)
    sums = (feature_count, 4 * half, HALF)
    operands = [codes, mine, other]
    in_specs = [
        pl.BlockSpec((joined, feature_count, length), lambda i: (i, 0, 0)),
        pl.BlockSpec((joined, half, length), lambda i: (i, 0, 0)),
        pl.BlockSpec((joined, half, length), lambda i: (i, 0, 0)),
    ]
    whole = pl.BlockSpec(sums, lambda i: (0, 0, 0))
    if before is not None:
        operands.append(before)
        in_specs.append(whole)
    return pl.pallas_call(
        functools.partial(hist_kernel, blocks // joined, feature_count, before is None, last),
        out_shape=shape(feature_count, BINS) if last else shape(*sums),
        grid=(blocks // joined,),
        in_specs=in_specs,
        out_specs=pl.BlockSpec((feature_count, BINS), lambda i: (0, 0)) if last else whole,
        scratch_shapes=[pltpu.VMEM(sums, f32)] if last else [],
        input_output_aliases={3: 0} if before is not None and not last else {},
        name="hist",
        compiler_params=pltpu.CompilerParams(dimension_semantics=("arbitrary",), vmem_limit_bytes=20 << 20),
        cost_estimate=pl.CostEstimate(
            flops=blocks * feature_count * 2 * (4 * half) * HALF * length * 4,
            bytes_accessed=blocks * (feature_count + 2 * half) * length * 2,
            transcendentals=0,
        ),
    )(*operands)


def call(kernel, out_shape, name, *operands, place=False):
    single = isinstance(out_shape, jax.ShapeDtypeStruct)
    return pl.pallas_call(
        kernel,
        out_shape=out_shape,
        in_specs=([SMEM] if place else []) + [VMEM] * (len(operands) - place),
        out_specs=VMEM if single else (VMEM,) * len(out_shape),
        name=name,
        compiler_params=pltpu.CompilerParams(vmem_limit_bytes=12 << 20),
    )(*operands)


def shape(*dims, dtype=f32):
    return jax.ShapeDtypeStruct(dims, dtype)


VMEM = pl.BlockSpec(memory_space=pltpu.VMEM)
SMEM = pl.BlockSpec(memory_space=pltpu.SMEM)


def ring(devices, d):
    return [(i, (i + 4 * d) % devices) for i in range(devices)]


def flip(devices, d):
    return [(i, i ^ d) for i in range(devices)]


def swap(x):
    return lax.ppermute(x, "feat", [(0, 1), (1, 0)])


def pick(x, index, axis):
    return lax.dynamic_index_in_dim(x, index, axis, False)


def send_planes(codes, devices):
    planes = devices // 4
    plane = lax.axis_index("tm") // 4
    codes = codes.reshape(planes, 4, -1, codes.shape[1])
    held = [pick(codes, plane, 0)]
    for d in range(1, planes):
        held.append(lax.ppermute(pick(codes, (plane + d) % planes, 0), "tm", ring(devices, d)))
    return held


def spread(held, plane, pairs, devices):
    planes = devices // 4
    here = lax.axis_index("tm") % 4
    column = [lax.ppermute(pairs, "tm", ring(devices, d)) for d in range(1, planes)]
    beside = [lax.ppermute(pairs, "tm", flip(devices, d)) for d in range(1, 4)]
    own = pick(held[0], here, 0)
    near = jnp.stack([pick(h, here, 0) for h in held[1:]])
    far = [
        lax.ppermute(jnp.stack([pick(h, here ^ d, 0) for h in held[1:]]), "tm", flip(devices, d))
        for d in range(1, 4)
    ]
    column, beside, pairs = lax.optimization_barrier((column, beside, pairs))
    column = jnp.stack(column)
    there = [lax.ppermute(column, "tm", flip(devices, d)) for d in range(1, 4)]
    other = swap(column)
    beside = jnp.stack([pairs] + beside)
    sums = histogram(jnp.stack([own] + plane), beside, swap(beside), None, False)
    cut = planes - 2
    sums = histogram(near[:cut], column[:cut], other[:cut], sums, False)
    there[0], sums = lax.optimization_barrier((there[0], sums))
    back = [swap(x) for x in there]
    sums = histogram(near[cut:], column[cut:], other[cut:], sums, False)
    for d in range(1, 4):
        sums = histogram(far[d - 1], there[d - 1], back[d - 1], sums, d == 3)
    return sums


def spread_any(codes, pairs):
    rows = lax.all_gather(pairs, "tm")
    return histogram(codes, rows, swap(rows), None, True)


def on_device(devices, margins, events, tie_group, in_node, bins):
    endpoints, length = margins.shape
    here = lax.axis_index("tm")[None].astype(jnp.int32)
    mine = bins.shape[0] // devices
    rows = shape(endpoints, length)
    narrow = shape(endpoints, length, dtype=bf16)

    def exchange(total):
        return lax.all_to_all(total, "tm", 0, 0)

    risk, total = call(risk_kernel, (rows, shape(devices, endpoints, LANES)), "risk", margins)
    parts = exchange(total)
    local = call(open_kernel, rows, "opens", risk, tie_group)
    bins, local = lax.optimization_barrier((bins, local))
    codes = bins.astype(bf16)
    blocked = devices == 16
    if blocked:
        codes = send_planes(codes, devices)
    else:
        codes = lax.all_to_all(codes.reshape(devices, mine, length), "tm", 0, 0)
    first, second, total = call(
        event_kernel, (rows, rows, shape(devices, 1, LANES)), "events",
        here, local, parts, events, place=True,
    )
    parts = exchange(total)
    if blocked:
        column = lax.axis_index("tm") % 4
        aside, second = lax.optimization_barrier((codes[0], second))
        plane = [lax.ppermute(pick(aside, column ^ d, 0), "tm", flip(devices, d)) for d in range(1, 4)]
    first, second = call(close_kernel, (rows, rows), "closes", first, second, tie_group)
    codes, parts = lax.optimization_barrier((codes, parts))
    grad, hess, pairs = call(
        grad_kernel, (narrow, narrow, shape(2 * endpoints, length, dtype=bf16)), "grads",
        here, margins, events, in_node, first, second, parts, place=True,
    )
    if blocked:
        plane, pairs = lax.optimization_barrier((plane, pairs))
    gain = spread(codes, plane, pairs, devices) if blocked else spread_any(codes, pairs)
    return (grad, hess, gain[None])


def solution(mesh):
    in_specs = (P("feat", "tm"), P("feat", "tm"), P("tm"), P("tm"), P("feat", "tm"))
    out_specs = (P("feat", "tm"), P("feat", "tm"), P("feat", "tm", None))
    return jax.shard_map(
        functools.partial(on_device, mesh.shape["tm"]),
        mesh=mesh, in_specs=in_specs, out_specs=out_specs, check_vma=False,
    )
```
